512 devices in a mesh: dp: 16 (over z, core), ctx: 8 (over x, y_lo), mp: 4 (over y_hi).
Axes of the slice: x: 4, y: 8 (y_hi: 4, y_lo: 2; y = y_hi * 2 + y_lo), z: 8, core: 2. Of those that a mesh axis runs over, the one named last changes fastest.
Arguments:
- queries: bfloat16 [16, 1024, 4096], P('dp', 'ctx', 'mp'), may hold values from -1.6953125 to 1.6953125
- keys: bfloat16 [16, 1024, 4096], P('dp', 'ctx', 'mp'), may hold values from -1.6953125 to 1.6953125
- values: bfloat16 [16, 1024, 4096], P('dp', 'ctx', 'mp'), may hold values from -6 to 6
- cross_queries: bfloat16 [16, 1024, 4096], P('dp', 'ctx', 'mp'), may hold values from -1.6953125 to 1.6953125
- encoded_bank: bfloat16 [16, 64, 64, 896], P('dp', 'ctx'), may hold values from -6 to 6
- key_weight: bfloat16 [896, 4096], P(('dp', 'ctx'), 'mp'), may hold values from -0.1875 to 0.1875
- value_weight: bfloat16 [896, 4096], P(('dp', 'ctx'), 'mp'), may hold values from -0.1875 to 0.1875
- owner_ids: int32 [16, 16, 2], P('dp', 'ctx'), may hold values from 0 to 15, as said below
- unit_ids: int32 [16, 16, 2], P('dp', 'ctx'), may hold values from 0 to 6
- lengths: int32 [16], P('dp'), may hold values from 64 to 1024
Outputs:
- self_core: bfloat16 [16, 1024, 4096], P('dp', 'ctx', 'mp')
- cross_core: bfloat16 [16, 1024, 4096], P('dp', 'ctx', 'mp')
The draws below stay inside these ranges and needn't reach their ends.
Inputs may be any that keep to these rules, and one draw needn't show every extreme that they name: `owner_ids`: among the 4 neighbours of the spans of one device (aligned blocks of 2 spans), no owner is named more than once.
All inputs are finite; a program needn't handle non-finite values.
Results may differ from the reference program's by a relative error of at most 0.006.
Values may be sent and summed in bfloat16 or wider, within the bound.
No kernel may reach another device: no remote copies, remote signals or barrier semaphores. Data moves between devices by JAX's collectives and lax.ppermute only.
A program may use at most 64 MiB of HBM per device.

```python
import math
import jax
import jax.numpy as jnp
import numpy as np
from jax import lax

HEADS = 32
HD = 128
ENC = 896
SPAN = 64
NBR = 2
SPANS_DEV = 2
SEQ = 1024
BANK_UNITS = 8
N_DP = 16
N_CTX = 8


def draw_owner_ids(key, part):
    device_count = N_DP * N_CTX
    request_total = SPANS_DEV * NBR

    def one_device(device_key):
        first_key, second_key = jax.random.split(device_key)
        permuted = jax.random.permutation(first_key, N_DP)
        picks = permuted[jnp.arange(request_total) % N_DP]
        shuffled = jax.random.permutation(second_key, request_total)
        return picks[shuffled]
    device_keys = jax.random.split(key, device_count)
    owners = jax.vmap(one_device)(device_keys)
    return owners.reshape(N_DP, N_CTX * SPANS_DEV, NBR).astype(jnp.int32)


def set_ends(entries, own_key, smallest, top_value):
    spot = [jax.random.randint(jax.random.fold_in(own_key, axis), (), 0, length) for axis, length in enumerate(entries.shape)]
    longest = entries.shape.index(max(entries.shape))
    beside = spot[:longest] + [(spot[longest] + 1) % entries.shape[longest]] + spot[longest + 1:]
    return entries.at[tuple(spot)].set(smallest).at[tuple(beside)].set(top_value)


def levels(rng, extent, cuts, least, high):
    factor_of, own = 1.0, jax.random.fold_in(rng, 6)
    for dim, blocks in cuts:
        steps = jnp.exp(jax.random.uniform(jax.random.fold_in(own, dim), (blocks,), jnp.float32, least / len(cuts), high / len(cuts)))
        factor_of = factor_of * jnp.repeat(steps, extent[dim] // blocks).reshape([-1 if axis == dim else 1 for axis in range(len(extent))])
    return factor_of


def rank_table(count, skew):
    weights = [(1 << 20) // math.isqrt(standing ** skew) + 1 for standing in range(1, count + 1)]
    width = 1 + sum(weights) // (1 << 30)
    return np.cumsum(np.array([max(1, weight // width) for weight in weights]))


def skewed_ids(rng, shape, amount, lean):
    grid = rank_table(amount, lean)
    lot = jax.random.randint(jax.random.fold_in(rng, 1), shape, 0, int(grid[amount - 1]))
    grade = jnp.searchsorted(jnp.asarray(grid, jnp.int32), lot, side="right")
    return jax.random.permutation(jax.random.fold_in(rng, 2), amount)[grade].astype(jnp.int32)


def noise(rng, dims, spread, bound, cuts=(), kind=jnp.bfloat16):
    gain = levels(rng, dims, cuts, -0.22, 0.18) if cuts else 1.0
    drawn = jax.random.normal(rng, dims, jnp.float32) * spread * gain
    return jnp.minimum(jnp.maximum(drawn, -bound), bound).astype(kind)


def setup_inputs(seed: int = 0) -> dict:
    key_list = jax.random.split(jax.random.key(seed), 11)
    return {
        "queries": jnp.clip(jax.random.uniform(key_list[0], (N_DP, SEQ, HEADS * HD), jnp.float32, -1.6953125, 1.6953125) * levels(key_list[0], (N_DP, SEQ, HEADS * HD), ((0, 16), (1, 8), (2, 4)), -0.4, 0.0), -1.6953125, 1.6953125).astype(jnp.bfloat16),
        "keys": jnp.clip(jax.random.uniform(key_list[1], (N_DP, SEQ, HEADS * HD), jnp.float32, -1.6953125, 1.6953125) * levels(key_list[1], (N_DP, SEQ, HEADS * HD), ((0, 16), (1, 8), (2, 4)), -0.4, 0.0), -1.6953125, 1.6953125).astype(jnp.bfloat16),
        "values": noise(key_list[2], (N_DP, SEQ, HEADS * HD), 1.0, 6.0, ((0, 16), (1, 8), (2, 4))),
        "cross_queries": jnp.clip(jax.random.uniform(key_list[3], (N_DP, SEQ, HEADS * HD), jnp.float32, -1.6953125, 1.6953125) * levels(key_list[3], (N_DP, SEQ, HEADS * HD), ((0, 16), (1, 8), (2, 4)), -0.4, 0.0), -1.6953125, 1.6953125).astype(jnp.bfloat16),
        "encoded_bank": noise(key_list[4], (N_DP, N_CTX * BANK_UNITS, SPAN, ENC), 1.0, 6.0, ((0, 16), (1, 8))),
        "key_weight": noise(key_list[5], (ENC, HEADS * HD), ENC ** -0.5, 0.1875, ((0, 128), (1, 4))),
        "value_weight": noise(key_list[6], (ENC, HEADS * HD), ENC ** -0.5, 0.1875, ((0, 128), (1, 4))),
        "owner_ids": draw_owner_ids(jax.random.fold_in(key_list[10], 71), 0),
        "unit_ids": set_ends(skewed_ids(key_list[8], (N_DP, N_CTX * SPANS_DEV, NBR), BANK_UNITS - 1, 2), jax.random.fold_in(key_list[8], 3), 0, (BANK_UNITS - 1) - 1).astype(jnp.int32),
        "lengths": set_ends(jax.random.randint(key_list[9], (N_DP,), SPAN, SEQ + 1), jax.random.fold_in(key_list[9], 1), SPAN, SEQ).astype(jnp.int32),
    }


def split_heads(rows):
    return jnp.transpose(rows.reshape(rows.shape[0], HEADS, HD), (1, 0, 2))

def self_dossier(query_rows, key_rows, value_rows, dossier_length):
    seq_total = query_rows.shape[0]
    positions = jnp.arange(seq_total, dtype=jnp.int32)
    causal = positions[None, :] <= positions[:, None]

    def one_head(parts):
        query_head, key_head, value_head = parts
        scores = jnp.dot(query_head, key_head.T, preferred_element_type=jnp.float32) * (1.0 / math.sqrt(HD))
        weights = jnp.where(causal, jnp.exp(scores), 0.0)
        sums = jnp.dot(weights.astype(jnp.bfloat16), value_head, preferred_element_type=jnp.float32)
        return sums / lax.optimization_barrier(jnp.sum(weights, axis=1, keepdims=True))
    heads = lax.map(one_head, (split_heads(query_rows), split_heads(key_rows), split_heads(value_rows)))
    joined = jnp.transpose(heads, (1, 0, 2)).reshape(seq_total, HEADS * HD)
    return jnp.where((positions < dossier_length)[:, None], joined, 0.0).astype(jnp.bfloat16)

def cross_dossier(query_rows, owners, units, dossier_length, encoded_bank, key_weight, value_weight):
    seq_total = query_rows.shape[0]
    span_total = seq_total // SPAN
    positions = jnp.arange(seq_total, dtype=jnp.int32)

    def one_span(parts):
        span_number, span_owners, span_units, span_queries = parts
        device_column = span_number // SPANS_DEV
        pieces = []
        for neighbour in range(NBR):
            owner_bank = encoded_bank[span_owners[neighbour]]
            first_unit = (device_column * BANK_UNITS + span_units[neighbour]).astype(jnp.int32)
            pieces.append(lax.dynamic_slice_in_dim(owner_bank, first_unit, 2, 0).reshape(2 * SPAN, ENC))
        retrieved = jnp.concatenate(pieces, axis=0)
        key_proj = jnp.dot(retrieved, key_weight, preferred_element_type=jnp.float32).reshape(-1, HEADS, HD)
        key_scale = lax.rsqrt(lax.optimization_barrier(jnp.mean(key_proj * key_proj, axis=2, keepdims=True)) + 1e-06)
        key_norm = lax.optimization_barrier((key_proj * key_scale).astype(jnp.bfloat16))
        value_proj = lax.optimization_barrier(jnp.dot(retrieved, value_weight, preferred_element_type=jnp.float32).astype(jnp.bfloat16))
        value_heads = value_proj.reshape(-1, HEADS, HD)
        query_heads = span_queries.reshape(SPAN, HEADS, HD)
        scores = jnp.einsum('qhd,khd->hqk', query_heads.astype(jnp.float32), key_norm.astype(jnp.float32), precision=lax.Precision.HIGHEST) * (1.0 / math.sqrt(HD))
        weights = jnp.exp(scores)
        rounded = lax.optimization_barrier(weights.astype(jnp.bfloat16))
        sums = jnp.einsum('hqk,khd->qhd', rounded.astype(jnp.float32), value_heads.astype(jnp.float32), precision=lax.Precision.HIGHEST)
        result = sums / jnp.transpose(lax.optimization_barrier(jnp.sum(weights, axis=2)))[:, :, None]
        return result.reshape(SPAN, HEADS * HD)
    span_numbers = jnp.arange(span_total, dtype=jnp.int32)
    outputs = lax.map(one_span, (span_numbers, owners, units, query_rows.reshape(span_total, SPAN, HEADS * HD)))
    joined = outputs.reshape(seq_total, HEADS * HD)
    return jnp.where((positions < dossier_length)[:, None], joined, 0.0).astype(jnp.bfloat16)

def reference(queries, keys, values, cross_queries, encoded_bank, key_weight, value_weight, owner_ids, unit_ids, lengths):

    def one_dossier(parts):
        query_rows, key_rows, value_rows, cross_rows, owners, units, dossier_length = parts
        first = self_dossier(query_rows, key_rows, value_rows, dossier_length)
        second = cross_dossier(cross_rows, owners, units, dossier_length, encoded_bank, key_weight, value_weight)
        return (first, second)
    self_core, cross_core = lax.map(one_dossier, (queries, keys, values, cross_queries, owner_ids, unit_ids, lengths))
    return (self_core, cross_core)
```

```python
import functools
import math

import jax
import jax.numpy as jnp
from jax import lax
from jax.experimental import pallas as pl
from jax.experimental.pallas import tpu as pltpu
from jax.sharding import Mesh, PartitionSpec as P

HD = 128
SPAN = 64
NBR = 2
SCALE = 1.0 / math.sqrt(HD)
BF = jnp.bfloat16
F32 = jnp.float32
NT = (((1,), (1,)), ((), ()))


def pack_body(q_ref, k_ref, v_ref, o_ref):
    for h in range(o_ref.shape[0]):
        cols = slice(h * HD, (h + 1) * HD)
        o_ref[h, 0] = q_ref[0, :, cols]
        o_ref[h, 1] = k_ref[0, :, cols]
        o_ref[h, 2] = v_ref[0, :, cols]


def pack_heads(q, k, v):
    rows, width = q.shape[1:]
    return pl.pallas_call(
        pack_body,
        out_shape=jax.ShapeDtypeStruct((width // HD, 3, rows, HD), q.dtype),
        name="pack_heads",
    )(q, k, v)


def self_body(len_ref, x_ref, o_ref, k_ref, v_ref):
    blocks, _, rows, _ = x_ref.shape
    for j in range(blocks):
        k_ref[pl.ds(j * rows, rows), :] = x_ref[j, 1]
        v_ref[pl.ds(j * rows, rows), :] = x_ref[j, 2]
    length = len_ref[0]
    for i in range(blocks):
        width = (i + 1) * rows
        scores = lax.dot_general(
            x_ref[i, 0], k_ref[:width, :], NT, preferred_element_type=F32
        ) * SCALE
        row = lax.broadcasted_iota(jnp.int32, (rows, width), 0) + i * rows
        col = lax.broadcasted_iota(jnp.int32, (rows, width), 1)
        weights = jnp.where(col <= row, jnp.exp(scores), 0.0)
        sums = jnp.dot(weights.astype(BF), v_ref[:width, :], preferred_element_type=F32)
        result = sums / jnp.sum(weights, axis=1, keepdims=True)
        place = lax.broadcasted_iota(jnp.int32, (rows, HD), 0) + i * rows
        o_ref[i] = jnp.where(place < length, result, 0.0).astype(BF)


def self_attention(lengths, x):
    blocks, _, rows, _ = x.shape
    return pl.pallas_call(
        self_body,
        out_shape=jax.ShapeDtypeStruct((blocks, rows, HD), BF),
        in_specs=[
            pl.BlockSpec(memory_space=pltpu.SMEM),
            pl.BlockSpec(memory_space=pltpu.VMEM),
        ],
        scratch_shapes=[pltpu.VMEM((blocks * rows, HD), BF)] * 2,
        name="self_attention",
    )(lengths, x)


def offer_body(ids_ref, where_ref, bank_ref, o_ref, sem, *, asks):
    peers, part = o_ref.shape[0], o_ref.shape[1]
    me, piece = where_ref[0], where_ref[1]
    copies = []
    for r in range(peers):
        unit = jnp.int32(0)
        for t in range(asks):
            unit = jnp.where(ids_ref[r, t] == me, ids_ref[r, asks + t], unit)
        start = pl.multiple_of(unit * SPAN + piece * part, part)
        copies.append(
            pltpu.make_async_copy(bank_ref.at[pl.ds(start, part), :], o_ref.at[r], sem.at[r])
        )
        copies[-1].start()
    for copy in copies:
        copy.wait()


def offer_rows(ids, where, bank, part):
    peers, width = ids.shape
    return pl.pallas_call(
        functools.partial(offer_body, asks=width // 2),
        out_shape=jax.ShapeDtypeStruct((peers, part, bank.shape[1]), bank.dtype),
        in_specs=[
            pl.BlockSpec(memory_space=pltpu.SMEM),
            pl.BlockSpec(memory_space=pltpu.SMEM),
            pl.BlockSpec(memory_space=pl.ANY),
        ],
        out_specs=pl.BlockSpec(memory_space=pltpu.VMEM),
        scratch_shapes=[pltpu.SemaphoreType.DMA((peers,))],
        name="offer_rows",
    )(ids, where, bank)


def choose_body(own_ref, x_ref, o_ref, sem):
    copies = []
    for t in range(o_ref.shape[0]):
        copies.append(pltpu.make_async_copy(x_ref.at[own_ref[t]], o_ref.at[t], sem.at[t]))
        copies[-1].start()
    for copy in copies:
        copy.wait()


def choose_rows(owners, received):
    asks = owners.shape[0]
    return pl.pallas_call(
        choose_body,
        out_shape=jax.ShapeDtypeStruct((asks,) + received.shape[1:], received.dtype),
        in_specs=[
            pl.BlockSpec(memory_space=pltpu.SMEM),
            pl.BlockSpec(memory_space=pl.ANY),
        ],
        out_specs=pl.BlockSpec(memory_space=pltpu.VMEM),
        scratch_shapes=[pltpu.SemaphoreType.DMA((asks,))],
        name="choose_rows",
    )(owners, received)


def cross_body(
    pos_ref, r_ref, pick_ref, ka_ref, kb_ref, va_ref, vb_ref, q_ref, o_ref, rows_ref, *, parts
):
    spans = q_ref.shape[1] // SPAN
    total = r_ref.shape[0]
    half = pick_ref.shape[2]

    @pl.when(pl.program_id(0) == 0)
    def _():
        for side in range(2):
            rows_ref[:, side * half : (side + 1) * half] = jnp.dot(
                r_ref[...], pick_ref[side], preferred_element_type=F32
            ).astype(BF)

    def project(a_ref, b_ref):
        return jnp.dot(rows_ref[:, :half], a_ref[...], preferred_element_type=F32) + jnp.dot(
            rows_ref[:, half:], b_ref[...], preferred_element_type=F32
        )

    key_proj = project(ka_ref, kb_ref)
    value_proj = project(va_ref, vb_ref).astype(BF)
    start, length = pos_ref[0], pos_ref[1]
    for h in range(o_ref.shape[2] // HD):
        cols = slice(h * HD, (h + 1) * HD)
        keys = key_proj[:, cols]
        scale = lax.rsqrt(jnp.mean(keys * keys, axis=1, keepdims=True) + 1e-06)
        keys = (keys * scale).astype(BF).reshape(parts, spans, total // (parts * spans), HD)
        values = value_proj[:, cols].reshape(parts, spans, total // (parts * spans), HD)
        for s in range(spans):
            scores = lax.dot_general(
                q_ref[0, s * SPAN : (s + 1) * SPAN, cols],
                keys[:, s].reshape(total // spans, HD),
                NT,
                preferred_element_type=F32,
            ) * SCALE
            weights = jnp.exp(scores)
            sums = jnp.dot(
                weights.astype(BF),
                values[:, s].reshape(total // spans, HD),
                preferred_element_type=F32,
            )
            result = sums / jnp.sum(weights, axis=1, keepdims=True)
            place = lax.broadcasted_iota(jnp.int32, (SPAN, HD), 0) + (start + s * SPAN)
            o_ref[0, s * SPAN : (s + 1) * SPAN, cols] = jnp.where(
                place < length, result, 0.0
            ).astype(BF)


def cross_attention(pos, retrieved, pick, own_w, other_w, queries, parts):
    total, enc = retrieved.shape
    half, width = own_w.shape[0], own_w.shape[1] // 2
    wide = 2 * HD
    steps = width // wide
    rows = queries.shape[1]
    whole = lambda *shape: pl.BlockSpec(shape, lambda j: (0,) * len(shape))
    key_block = pl.BlockSpec((half, wide), lambda j: (0, j))
    value_block = pl.BlockSpec((half, wide), lambda j: (0, j + steps))
    tokens = pl.BlockSpec((1, rows, wide), lambda j: (0, 0, j))
    return pl.pallas_call(
        functools.partial(cross_body, parts=parts),
        grid=(steps,),
        out_shape=jax.ShapeDtypeStruct(queries.shape, BF),
        in_specs=[
            pl.BlockSpec(memory_space=pltpu.SMEM),
            whole(total, enc),
            whole(2, enc, half),
            key_block,
            key_block,
            value_block,
            value_block,
            tokens,
        ],
        out_specs=tokens,
        scratch_shapes=[pltpu.VMEM((total, 2 * half), BF)],
        name="cross_attention",
    )(pos, retrieved, pick, own_w, other_w, own_w, other_w, queries)


def spread(x, axis):
    copies = jnp.broadcast_to(x[None], (lax.axis_size(axis),) + x.shape)
    return lax.all_to_all(copies, axis, 0, 0, tiled=True)


def local(
    queries,
    keys,
    values,
    cross_queries,
    encoded_bank,
    key_weight,
    value_weight,
    owner_ids,
    unit_ids,
    lengths,
):
    dp = ("z", "core")
    n_z, n_core, n_ctx, n_mp = (lax.axis_size(a) for a in ("z", "core", "ctx", "mp"))
    core, ctx, piece = lax.axis_index("core"), lax.axis_index("ctx"), lax.axis_index("mp")
    rows, width = queries.shape[1:]
    enc = encoded_bank.shape[3]
    asks = owner_ids.shape[1] * NBR
    part = 2 * SPAN // n_mp

    ids = jnp.concatenate([owner_ids.reshape(asks), unit_ids.reshape(asks)])
    asked = spread(ids, dp)

    shard = jnp.concatenate([key_weight, value_weight], axis=1)
    depth = shard.shape[0]
    pad = -(-depth // 8) * 8
    shard = jnp.pad(shard, ((0, pad - depth), (0, 0)))
    column = spread(shard, "z").reshape(n_z * pad, 2 * width)

    packed = lax.all_to_all(pack_heads(queries, keys, values), "ctx", 0, 0, tiled=True)
    head = self_attention(lengths, packed)
    back = lax.all_to_all(head, "ctx", 0, 0, tiled=True)
    self_core = jnp.transpose(back, (1, 0, 2)).reshape(1, rows, width)

    where = jnp.stack([lax.axis_index(dp), piece]).astype(jnp.int32)
    offered = offer_rows(asked, where, encoded_bank.reshape(-1, enc), part)
    received = lax.all_to_all(offered, dp, 0, 0, tiled=True)
    mine = choose_rows(owner_ids.reshape(asks), received).reshape(asks * part, enc)
    retrieved = lax.all_gather(mine, "mp", axis=0, tiled=True)

    own_w = spread(column, "ctx").reshape(n_ctx * n_z * pad, 2 * width)
    other_w = lax.ppermute(own_w, "core", [(i, (i + 1) % n_core) for i in range(n_core)])

    half = n_ctx * n_z * pad
    j = lax.broadcasted_iota(jnp.int32, (n_core, enc, half), 2)
    side = lax.broadcasted_iota(jnp.int32, (n_core, enc, half), 0)
    e = lax.broadcasted_iota(jnp.int32, (n_core, enc, half), 1)
    i, z, c = j % pad, (j // pad) % n_z, j // (pad * n_z)
    source = ((z * n_core + (core + side) % n_core) * n_ctx + c) * depth + i
    pick = ((source == e) & (i < depth)).astype(BF)

    pos = jnp.stack([ctx * rows, lengths[0]]).astype(jnp.int32)
    cross_core = cross_attention(pos, retrieved, pick, own_w, other_w, cross_queries, n_mp)
    return self_core, cross_core


def solution(mesh):
    n_dp, n_ctx, n_mp = (mesh.shape[a] for a in ("dp", "ctx", "mp"))
    fine = Mesh(mesh.devices.reshape(n_dp // 2, 2, n_ctx, n_mp), ("z", "core", "ctx", "mp"))
    dp = ("z", "core")
    tokens = P(dp, "ctx", "mp")
    weight = P(("z", "core", "ctx"), "mp")
    in_specs = (
        tokens,
        tokens,
        tokens,
        tokens,
        P(dp, "ctx", None, None),
        weight,
        weight,
        P(dp, "ctx", None),
        P(dp, "ctx", None),
        P(dp),
    )
    return jax.shard_map(
        local, mesh=fine, in_specs=in_specs, out_specs=(tokens, tokens), check_vma=False
    )
```

```python
import functools
import math

import jax
import jax.numpy as jnp
from jax import lax
from jax.experimental import pallas as pl
from jax.experimental.pallas import tpu as pltpu
from jax.sharding import Mesh, PartitionSpec as P

HD = 128
SPAN = 64
NBR = 2
SCALE = 1.0 / math.sqrt(HD)
BF = jnp.bfloat16
F32 = jnp.float32
NT = (((1,), (1,)), ((), ()))


def pack_body(q_ref, k_ref, v_ref, o_ref):
    for h in range(o_ref.shape[0]):
        cols = slice(h * HD, (h + 1) * HD)
        o_ref[h, 0] = q_ref[0, :, cols]
        o_ref[h, 1] = k_ref[0, :, cols]
        o_ref[h, 2] = v_ref[0, :, cols]


def pack_heads(q, k, v):
    rows, width = q.shape[1:]
    return pl.pallas_call(
        pack_body,
        out_shape=jax.ShapeDtypeStruct((width // HD, 3, rows, HD), q.dtype),
        name="pack_heads",
    )(q, k, v)


def self_body(len_ref, x_ref, o_ref, k_ref, v_ref):
    blocks, _, rows, _ = x_ref.shape
    for j in range(blocks):
        k_ref[pl.ds(j * rows, rows), :] = x_ref[j, 1]
        v_ref[pl.ds(j * rows, rows), :] = x_ref[j, 2]
    length = len_ref[0]
    for i in range(blocks):
        width = (i + 1) * rows
        scores = lax.dot_general(
            x_ref[i, 0], k_ref[:width, :], NT, preferred_element_type=F32
        ) * SCALE
        row = lax.broadcasted_iota(jnp.int32, (rows, width), 0) + i * rows
        col = lax.broadcasted_iota(jnp.int32, (rows, width), 1)
        weights = jnp.where(col <= row, jnp.exp(scores), 0.0)
        sums = jnp.dot(weights.astype(BF), v_ref[:width, :], preferred_element_type=F32)
        result = sums / jnp.sum(weights, axis=1, keepdims=True)
        place = lax.broadcasted_iota(jnp.int32, (rows, HD), 0) + i * rows
        o_ref[i] = jnp.where(place < length, result, 0.0).astype(BF)


def self_attention(lengths, x):
    blocks, _, rows, _ = x.shape
    return pl.pallas_call(
        self_body,
        out_shape=jax.ShapeDtypeStruct((blocks, rows, HD), BF),
        in_specs=[
            pl.BlockSpec(memory_space=pltpu.SMEM),
            pl.BlockSpec(memory_space=pltpu.VMEM),
        ],
        scratch_shapes=[pltpu.VMEM((blocks * rows, HD), BF)] * 2,
        name="self_attention",
    )(lengths, x)


def offer_body(ids_ref, where_ref, bank_ref, o_ref, *, asks):
    peers, part = o_ref.shape[0], o_ref.shape[1]
    me, piece, core = where_ref[0], where_ref[1], where_ref[2]
    for z in range(peers // 2):
        for side in range(2):
            unit = jnp.int32(0)
            for t in range(asks):
                at = (2 * side) * asks + t
                unit = jnp.where(ids_ref[z, at] == me, ids_ref[z, at + asks], unit)
            start = pl.multiple_of(unit * SPAN + piece * part, part)
            o_ref[2 * z + jnp.bitwise_xor(core, side)] = bank_ref[pl.ds(start, part), :]


def offer_rows(ids, where, bank, part):
    zs, width = ids.shape
    return pl.pallas_call(
        functools.partial(offer_body, asks=width // 4),
        out_shape=jax.ShapeDtypeStruct((2 * zs, part, bank.shape[1]), bank.dtype),
        in_specs=[
            pl.BlockSpec(memory_space=pltpu.SMEM),
            pl.BlockSpec(memory_space=pltpu.SMEM),
            pl.BlockSpec(memory_space=pltpu.VMEM),
        ],
        name="offer_rows",
    )(ids, where, bank)


def choose_body(own_ref, x_ref, o_ref):
    part = x_ref.shape[1]
    for t in range(o_ref.shape[0] // part):
        o_ref[t * part : (t + 1) * part, :] = x_ref[own_ref[t]]


def choose_rows(owners, received):
    asks = owners.shape[0]
    _, part, enc = received.shape
    return pl.pallas_call(
        choose_body,
        out_shape=jax.ShapeDtypeStruct((asks * part, enc), received.dtype),
        in_specs=[
            pl.BlockSpec(memory_space=pltpu.SMEM),
            pl.BlockSpec(memory_space=pltpu.VMEM),
        ],
        name="choose_rows",
    )(owners, received)


def cross_body(pos_ref, *refs):
    piece_refs, far_refs = refs[0:3], refs[3:5]
    pick_ref, ka_ref, kb_ref, va_ref, vb_ref, q_ref, o_ref, rows_ref = refs[5:]
    spans = q_ref.shape[1] // SPAN
    total = rows_ref.shape[0]
    each = total // spans
    half = pick_ref.shape[2]

    @pl.when(pl.program_id(0) == 0)
    def _():
        for side in range(2):
            cols = slice(side * half, (side + 1) * half)
            for p, piece in enumerate(piece_refs):
                part = jnp.dot(piece[...], pick_ref[side], preferred_element_type=F32)
                rows = part.shape[0] // spans
                for s in range(spans):
                    at = s * each + p * rows
                    rows_ref[at : at + rows, cols] = part[s * rows : (s + 1) * rows].astype(BF)
            for s, piece in enumerate(far_refs):
                part = jnp.dot(piece[...], pick_ref[side], preferred_element_type=F32)
                rows_ref[(s + 1) * each - part.shape[0] : (s + 1) * each, cols] = part.astype(BF)

    def project(a_ref, b_ref):
        return jnp.dot(rows_ref[:, :half], a_ref[...], preferred_element_type=F32) + jnp.dot(
            rows_ref[:, half:], b_ref[...], preferred_element_type=F32
        )

    key_proj = project(ka_ref, kb_ref)
    value_proj = project(va_ref, vb_ref).astype(BF)
    start, length = pos_ref[0], pos_ref[1]
    for h in range(o_ref.shape[2] // HD):
        cols = slice(h * HD, (h + 1) * HD)
        keys = key_proj[:, cols]
        scale = lax.rsqrt(jnp.mean(keys * keys, axis=1, keepdims=True) + 1e-06)
        keys = (keys * scale).astype(BF)
        values = value_proj[:, cols]
        for s in range(spans):
            own = slice(s * each, (s + 1) * each)
            scores = lax.dot_general(
                q_ref[0, s * SPAN : (s + 1) * SPAN, cols],
                keys[own],
                NT,
                preferred_element_type=F32,
            ) * SCALE
            weights = jnp.exp(scores)
            sums = jnp.dot(weights.astype(BF), values[own], preferred_element_type=F32)
            result = sums / jnp.sum(weights, axis=1, keepdims=True)
            place = lax.broadcasted_iota(jnp.int32, (SPAN, HD), 0) + (start + s * SPAN)
            o_ref[0, s * SPAN : (s + 1) * SPAN, cols] = jnp.where(
                place < length, result, 0.0
            ).astype(BF)


def cross_attention(pos, pieces, far, pick, own_w, other_w, queries):
    total = sum(p.shape[0] for p in pieces) + sum(p.shape[0] for p in far)
    half, width = own_w.shape[0], own_w.shape[1] // 2
    wide = 2 * HD
    steps = width // wide
    rows = queries.shape[1]
    whole = lambda x: pl.BlockSpec(x.shape, lambda j: (0,) * x.ndim)
    key_block = pl.BlockSpec((half, wide), lambda j: (0, j))
    value_block = pl.BlockSpec((half, wide), lambda j: (0, j + steps))
    tokens = pl.BlockSpec((1, rows, wide), lambda j: (0, 0, j))
    return pl.pallas_call(
        cross_body,
        grid=(steps,),
        out_shape=jax.ShapeDtypeStruct(queries.shape, BF),
        in_specs=[
            pl.BlockSpec(memory_space=pltpu.SMEM),
            *[whole(x) for x in pieces],
            *[whole(x) for x in far],
            whole(pick),
            key_block,
            key_block,
            value_block,
            value_block,
            tokens,
        ],
        out_specs=tokens,
        scratch_shapes=[pltpu.VMEM((total, 2 * half), BF)],
        name="cross_attention",
    )(pos, *pieces, *far, pick, own_w, other_w, own_w, other_w, queries)


def spread(x, axis):
    copies = jnp.broadcast_to(x[None], (lax.axis_size(axis),) + x.shape)
    return lax.all_to_all(copies, axis, 0, 0, tiled=True)


def shift(x, axis, by):
    n = lax.axis_size(axis)
    return lax.ppermute(x, axis, [(i, (i + by) % n) for i in range(n)])


def ring_gather(x, axis):
    rows = x.shape[0] // 2
    left, right = shift(x, axis, 1), shift(x, axis, -1)
    far = shift(left[:rows], axis, 1), shift(right[rows:], axis, -1)
    return (x, left, right), far


def local(
    queries,
    keys,
    values,
    cross_queries,
    encoded_bank,
    key_weight,
    value_weight,
    owner_ids,
    unit_ids,
    lengths,
):
    dp = ("z", "core")
    ctx_axes = ("x", "yl")
    core, x_at, y_at = (lax.axis_index(a) for a in ("core", "x", "yl"))
    n_z, n_x, n_y, n_mp = (lax.axis_size(a) for a in ("z", "x", "yl", "mp"))
    rows, width = queries.shape[1:]
    enc = encoded_bank.shape[3]
    asks = owner_ids.shape[1] * NBR
    part = 2 * SPAN // n_mp

    owners = owner_ids.reshape(asks)
    ids = jnp.concatenate([owners, unit_ids.reshape(asks)])
    ids = jnp.concatenate([ids, shift(ids, "core", 1)]).astype(BF)
    shard = jnp.concatenate([key_weight, value_weight], axis=1)
    depth = shard.shape[0]
    pad = -(-(depth + 1) // 8) * 8
    last = jnp.pad(ids[None], ((pad - depth - 1, 0), (0, 2 * width - ids.shape[0])))
    column = spread(jnp.concatenate([shard, last], axis=0), "z")
    asked = column[:, pad - 1, : ids.shape[0]].astype(jnp.int32)

    where = jnp.stack([lax.axis_index(dp), lax.axis_index("mp"), core]).astype(jnp.int32)
    offered = offer_rows(asked, where, encoded_bank.reshape(-1, enc), part)
    received = lax.all_to_all(offered, dp, 0, 0, tiled=True)
    pieces, far = ring_gather(choose_rows(owners, received), "mp")

    column = column.reshape(n_z * pad, 2 * width)
    column = jnp.concatenate([column, shift(column, "yl", 1)], axis=0)
    w_pieces, w_far = ring_gather(column, "x")
    own_w = jnp.concatenate([*w_pieces, *w_far], axis=0)
    other_w = shift(own_w, "core", 1)

    packed = lax.all_to_all(pack_heads(queries, keys, values), ctx_axes, 0, 0, tiled=True)
    head = self_attention(lengths, packed)
    back = lax.all_to_all(head, ctx_axes, 0, 0, tiled=True)
    self_core = jnp.transpose(back, (1, 0, 2)).reshape(1, rows, width)

    half = own_w.shape[0]
    block = n_y * n_z * pad
    j = jnp.arange(half, dtype=jnp.int32)
    ring = j // block
    x = jnp.where(ring == 1, x_at + n_x - 1, x_at + jnp.where(ring == 3, 2, jnp.where(ring == 2, 1, 0)))
    y = jnp.bitwise_xor(y_at, (j // (n_z * pad)) & 1)
    ctx = (x & (n_x - 1)) * n_y + y
    i, z = j & (pad - 1), (j // pad) & (n_z - 1)
    source = ((z * 2 + jnp.stack([core, 1 - core])[:, None]) * (n_x * n_y) + ctx) * depth + i
    source = jnp.where(i < depth, source, -1)
    pick = (source[:, None, :] == lax.broadcasted_iota(jnp.int32, (2, enc, half), 1)).astype(BF)

    pos = jnp.stack([(x_at * n_y + y_at) * rows, lengths[0]]).astype(jnp.int32)
    cross_core = cross_attention(pos, pieces, far, pick, own_w, other_w, cross_queries)
    return self_core, cross_core


def solution(mesh):
    n_dp, n_ctx, n_mp = (mesh.shape[a] for a in ("dp", "ctx", "mp"))
    devices = mesh.devices.reshape(n_dp // 2, 2, n_ctx // 2, 2, n_mp)
    fine = Mesh(devices, ("z", "core", "x", "yl", "mp"))
    dp, ctx = ("z", "core"), ("x", "yl")
    tokens = P(dp, ctx, "mp")
    weight = P(dp + ctx, "mp")
    in_specs = (
        tokens,
        tokens,
        tokens,
        tokens,
        P(dp, ctx, None, None),
        weight,
        weight,
        P(dp, ctx, None),
        P(dp, ctx, None),
        P(dp),
    )
    return jax.shard_map(
        local, mesh=fine, in_specs=in_specs, out_specs=(tokens, tokens), check_vma=False
    )
```

```python
import math

import jax
import jax.numpy as jnp
from jax import lax
from jax.experimental import pallas as pl
from jax.experimental.pallas import tpu as pltpu
from jax.sharding import Mesh, PartitionSpec as P


HD = 128
SPAN = 64
NBR = 2
SCALE = 1.0 / math.sqrt(HD)
BF = jnp.bfloat16
F32 = jnp.float32
NT = (((1,), (1,)), ((), ()))


def pack_body(q_ref, k_ref, v_ref, o_ref):
    for h in range(o_ref.shape[0]):
        cols = slice(h * HD, (h + 1) * HD)
        o_ref[h, 0] = q_ref[0, :, cols]
        o_ref[h, 1] = k_ref[0, :, cols]
        o_ref[h, 2] = v_ref[0, :, cols]


def pack_heads(q, k, v):
    rows, width = q.shape[1:]
    return pl.pallas_call(
        pack_body,
        out_shape=jax.ShapeDtypeStruct((width // HD, 3, rows, HD), q.dtype),
        name="pack_heads",
    )(q, k, v)


def self_body(len_ref, x_ref, o_ref, k_ref, v_ref):
    blocks, _, rows, _ = x_ref.shape
    for j in range(blocks):
        k_ref[pl.ds(j * rows, rows), :] = x_ref[j, 1]
        v_ref[pl.ds(j * rows, rows), :] = x_ref[j, 2]
    length = len_ref[0]
    for i in range(blocks):
        width = (i + 1) * rows
        scores = lax.dot_general(
            x_ref[i, 0], k_ref[:width, :], NT, preferred_element_type=F32
        ) * SCALE
        row = lax.broadcasted_iota(jnp.int32, (rows, width), 0) + i * rows
        col = lax.broadcasted_iota(jnp.int32, (rows, width), 1)
        weights = jnp.where(col <= row, jnp.exp(scores), 0.0)
        sums = jnp.dot(weights.astype(BF), v_ref[:width, :], preferred_element_type=F32)
        result = sums / jnp.sum(weights, axis=1, keepdims=True)
        place = lax.broadcasted_iota(jnp.int32, (rows, HD), 0) + i * rows
        o_ref[i] = jnp.where(place < length, result, 0.0).astype(BF)


def self_attention(lengths, x):
    blocks, _, rows, _ = x.shape
    return pl.pallas_call(
        self_body,
        out_shape=jax.ShapeDtypeStruct((blocks, rows, HD), BF),
        in_specs=[
            pl.BlockSpec(memory_space=pltpu.SMEM),
            pl.BlockSpec(memory_space=pltpu.VMEM),
        ],
        scratch_shapes=[pltpu.VMEM((blocks * rows, HD), BF)] * 2,
        name="self_attention",
    )(lengths, x)


def offer_body(ids_ref, where_ref, bank_ref, o_ref):
    peers, part = o_ref.shape[0], o_ref.shape[1]
    asks = ids_ref.shape[1] // 4
    me, piece, core = where_ref[0], where_ref[1], where_ref[2]
    for z in range(peers // 2):
        for side in range(2):
            unit = jnp.int32(0)
            for t in range(asks):
                at = side * 2 * asks + (t // NBR) * 2 * NBR + t % NBR
                unit = jnp.where(ids_ref[z, at] == me, ids_ref[z, at + NBR], unit)
            start = pl.multiple_of(unit * SPAN + piece * part, part)
            o_ref[2 * z + jnp.bitwise_xor(core, side)] = bank_ref[pl.ds(start, part), :]


def offer_rows(ids, where, bank, part):
    zs = ids.shape[0]
    return pl.pallas_call(
        offer_body,
        out_shape=jax.ShapeDtypeStruct((2 * zs, part, bank.shape[1]), bank.dtype),
        in_specs=[
            pl.BlockSpec(memory_space=pltpu.SMEM),
            pl.BlockSpec(memory_space=pltpu.SMEM),
            pl.BlockSpec(memory_space=pltpu.VMEM),
        ],
        name="offer_rows",
    )(ids, where, bank)


def choose_body(own_ref, x_ref, o_ref):
    part = x_ref.shape[1]
    for t in range(o_ref.shape[0] // part):
        o_ref[t * part : (t + 1) * part, :] = x_ref[own_ref[0, t // NBR, t % NBR]]


def choose_rows(owners, received):
    asks = owners.shape[1] * owners.shape[2]
    _, part, enc = received.shape
    return pl.pallas_call(
        choose_body,
        out_shape=jax.ShapeDtypeStruct((asks * part, enc), received.dtype),
        in_specs=[
            pl.BlockSpec(memory_space=pltpu.SMEM),
            pl.BlockSpec(memory_space=pltpu.VMEM),
        ],
        name="choose_rows",
    )(owners, received)


def stage_body(own_ref, other_ref, k_ref, v_ref, o_ref):
    copies, rows, width = o_ref.shape
    depth, half = k_ref.shape
    lane = lax.broadcasted_iota(jnp.int32, (1, HD), 1)
    spans, each = own_ref.shape[1:]
    last = jnp.zeros((1, HD), F32)
    for side, ref in enumerate((own_ref, other_ref)):
        for s in range(spans):
            for t in range(each):
                at = (side * spans + s) * each + t
                last = jnp.where(lane == at, ref[0, s, t].astype(F32), last)
    pad = jnp.zeros((rows - depth, HD), F32)
    row = lax.broadcasted_iota(jnp.int32, pad.shape, 0)
    tail = jnp.where(row == rows - depth - 1, last, pad)
    for c in range(width // HD):
        src, at = (k_ref, c * HD) if c * HD < half else (v_ref, c * HD - half)
        top = src[:, at : at + HD].astype(F32)
        end = tail if c == 0 else pad
        block = jnp.concatenate([top, end], axis=0).astype(BF)
        for n in range(copies):
            o_ref[n, :, c * HD : (c + 1) * HD] = block


def stage_weights(ids, other_ids, key_weight, value_weight, copies):
    depth, width = key_weight.shape
    rows = -(-(depth + 1) // 8) * 8
    smem, vmem = pl.BlockSpec(memory_space=pltpu.SMEM), pl.BlockSpec(memory_space=pltpu.VMEM)
    return pl.pallas_call(
        stage_body,
        out_shape=jax.ShapeDtypeStruct((copies, rows, 2 * width), BF),
        in_specs=[smem, smem, vmem, vmem],
        name="stage_weights",
    )(ids, other_ids, key_weight, value_weight)


def cross_body(pos_ref, *refs):
    piece_refs, far_refs = refs[0:3], refs[3:5]
    pick_ref, ka_ref, kb_ref, va_ref, vb_ref, q_ref, o_ref, rows_ref = refs[5:]
    spans = q_ref.shape[1] // SPAN
    total = rows_ref.shape[0]
    each = total // spans
    half = pick_ref.shape[2]

    @pl.when(pl.program_id(0) == 0)
    def _():
        for side in range(2):
            cols = slice(side * half, (side + 1) * half)
            for p, piece in enumerate(piece_refs):
                part = jnp.dot(piece[...], pick_ref[side], preferred_element_type=F32)
                rows = part.shape[0] // spans
                for s in range(spans):
                    at = s * each + p * rows
                    rows_ref[at : at + rows, cols] = part[s * rows : (s + 1) * rows].astype(BF)
            for s, piece in enumerate(far_refs):
                part = jnp.dot(piece[...], pick_ref[side], preferred_element_type=F32)
                rows_ref[(s + 1) * each - part.shape[0] : (s + 1) * each, cols] = part.astype(BF)

    def project(a_ref, b_ref):
        return jnp.dot(rows_ref[:, :half], a_ref[...], preferred_element_type=F32) + jnp.dot(
            rows_ref[:, half:], b_ref[...], preferred_element_type=F32
        )

    key_proj = project(ka_ref, kb_ref)
    value_proj = project(va_ref, vb_ref).astype(BF)
    start, length = pos_ref[0], pos_ref[1]
    for h in range(o_ref.shape[2] // HD):
        cols = slice(h * HD, (h + 1) * HD)
        keys = key_proj[:, cols]
        scale = lax.rsqrt(jnp.mean(keys * keys, axis=1, keepdims=True) + 1e-06)
        keys = (keys * scale).astype(BF)
        values = value_proj[:, cols]
        for s in range(spans):
            own = slice(s * each, (s + 1) * each)
            scores = lax.dot_general(
                q_ref[0, s * SPAN : (s + 1) * SPAN, cols],
                keys[own],
                NT,
                preferred_element_type=F32,
            ) * SCALE
            weights = jnp.exp(scores)
            sums = jnp.dot(weights.astype(BF), values[own], preferred_element_type=F32)
            result = sums / jnp.sum(weights, axis=1, keepdims=True)
            place = lax.broadcasted_iota(jnp.int32, (SPAN, HD), 0) + (start + s * SPAN)
            o_ref[0, s * SPAN : (s + 1) * SPAN, cols] = jnp.where(
                place < length, result, 0.0
            ).astype(BF)


def cross_attention(pos, pieces, far, pick, own_w, other_w, queries):
    total = sum(p.shape[0] for p in pieces) + sum(p.shape[0] for p in far)
    half, width = own_w.shape[0], own_w.shape[1] // 2
    wide = 2 * HD
    steps = width // wide
    rows = queries.shape[1]
    whole = lambda x: pl.BlockSpec(x.shape, lambda j: (0,) * x.ndim)
    key_block = pl.BlockSpec((half, wide), lambda j: (0, j))
    value_block = pl.BlockSpec((half, wide), lambda j: (0, j + steps))
    tokens = pl.BlockSpec((1, rows, wide), lambda j: (0, 0, j))
    return pl.pallas_call(
        cross_body,
        grid=(steps,),
        out_shape=jax.ShapeDtypeStruct(queries.shape, BF),
        in_specs=[
            pl.BlockSpec(memory_space=pltpu.SMEM),
            *[whole(x) for x in pieces],
            *[whole(x) for x in far],
            whole(pick),
            key_block,
            key_block,
            value_block,
            value_block,
            tokens,
        ],
        out_specs=tokens,
        scratch_shapes=[pltpu.VMEM((total, 2 * half), BF)],
        name="cross_attention",
    )(pos, *pieces, *far, pick, own_w, other_w, own_w, other_w, queries)


def shift(x, axis, by):
    n = lax.axis_size(axis)
    return lax.ppermute(x, axis, [(i, (i + by) % n) for i in range(n)])


def local(
    queries,
    keys,
    values,
    cross_queries,
    encoded_bank,
    key_weight,
    value_weight,
    owner_ids,
    unit_ids,
    lengths,
):
    dp = ("z", "core")
    ctx_axes = ("x", "yl")
    core, x_at, y_at = (lax.axis_index(a) for a in ("core", "x", "yl"))
    n_z, n_x, n_y, n_mp = (lax.axis_size(a) for a in ("z", "x", "yl", "mp"))
    rows, width = queries.shape[1:]
    enc = encoded_bank.shape[3]
    asks = owner_ids.shape[1] * NBR
    part = 2 * SPAN // n_mp

    ids = jnp.concatenate([owner_ids, unit_ids], axis=2)
    staged = stage_weights(ids, shift(ids, "core", 1), key_weight, value_weight, n_z)
    depth, pad = key_weight.shape[0], staged.shape[1]
    column = lax.all_to_all(staged, "z", 0, 0, tiled=True)
    asked = column[:, pad - 1, : 4 * asks].astype(jnp.int32)

    where = jnp.stack([lax.axis_index(dp), lax.axis_index("mp"), core]).astype(jnp.int32)
    offered = offer_rows(asked, where, encoded_bank.reshape(-1, enc), part)
    received = lax.all_to_all(offered, dp, 0, 0, tiled=True)
    mine = choose_rows(owner_ids, received)
    left = shift(mine, "mp", 1)
    right = shift(mine, "mp", -1)
    mid = mine.shape[0] // 2
    far_left = shift(left[:mid], "mp", 1)
    far_right = shift(right[mid:], "mp", -1)
    pieces, far = (mine, left, right), (far_left, far_right)

    column = column.reshape(n_z * pad, 2 * width)
    beside = shift(column, "yl", 1)
    column = jnp.concatenate([column, beside], axis=0)
    w_left = shift(column, "x", 1)
    w_right = shift(column, "x", -1)
    w_far = shift(w_left, "x", 1)
    own_w = jnp.concatenate([column, w_left, w_right, w_far], axis=0)
    other_w = shift(own_w, "core", 1)

    heads = pack_heads(queries, keys, values)
    packed = lax.all_to_all(heads, ctx_axes, 0, 0, tiled=True)
    head = self_attention(lengths, packed)
    back = lax.all_to_all(head, ctx_axes, 0, 0, tiled=True)
    self_core = jnp.transpose(back, (1, 0, 2)).reshape(1, rows, width)

    half = own_w.shape[0]
    block = n_y * n_z * pad
    j = jnp.arange(half, dtype=jnp.int32)
    ring = j // block
    ahead = jnp.where(ring == 1, n_x - 1, jnp.where(ring == 2, 1, jnp.where(ring == 3, 2, 0)))
    y = jnp.bitwise_xor(y_at, (j // (n_z * pad)) & 1)
    ctx = ((x_at + ahead) & (n_x - 1)) * n_y + y
    i, z = j & (pad - 1), (j // pad) & (n_z - 1)
    dp_at = z * 2 + jnp.stack([core, 1 - core])[:, None]
    source = (dp_at * (n_x * n_y) + ctx) * depth + i
    source = jnp.where(i < depth, source, -1)
    entry = lax.broadcasted_iota(jnp.int32, (2, enc, half), 1)
    pick = (source[:, None, :] == entry).astype(BF)

    pos = jnp.stack([(x_at * n_y + y_at) * rows, lengths[0]]).astype(jnp.int32)
    cross_core = cross_attention(pos, pieces, far, pick, own_w, other_w, cross_queries)
    return self_core, cross_core


def solution(mesh):
    n_dp, n_ctx, n_mp = (mesh.shape[a] for a in ("dp", "ctx", "mp"))
    devices = mesh.devices.reshape(n_dp // 2, 2, n_ctx // 2, 2, n_mp)
    fine = Mesh(devices, ("z", "core", "x", "yl", "mp"))
    dp, ctx = ("z", "core"), ("x", "yl")
    tokens = P(dp, ctx, "mp")
    weight = P(dp + ctx, "mp")
    in_specs = (
        tokens,
        tokens,
        tokens,
        tokens,
        P(dp, ctx, None, None),
        weight,
        weight,
        P(dp, ctx, None),
        P(dp, ctx, None),
        P(dp),
    )
    return jax.shard_map(
        local, mesh=fine, in_specs=in_specs, out_specs=(tokens, tokens), check_vma=False
    )
```

```python
import math

import jax
import jax.numpy as jnp
from jax import lax
from jax.experimental import pallas as pl
from jax.experimental.pallas import tpu as pltpu
from jax.sharding import Mesh, PartitionSpec as P


HD = 128
SPAN = 64
NBR = 2
SCALE = 1.0 / math.sqrt(HD)
BF = jnp.bfloat16
F32 = jnp.float32
NT = (((1,), (1,)), ((), ()))


def pack_body(q_ref, k_ref, v_ref, o_ref):
    for h in range(o_ref.shape[0]):
        cols = slice(h * HD, (h + 1) * HD)
        o_ref[h, 0] = q_ref[0, :, cols]
        o_ref[h, 1] = k_ref[0, :, cols]
        o_ref[h, 2] = v_ref[0, :, cols]


def pack_heads(q, k, v):
    rows, width = q.shape[1:]
    return pl.pallas_call(
        pack_body,
        out_shape=jax.ShapeDtypeStruct((width // HD, 3, rows, HD), q.dtype),
        name="pack_heads",
    )(q, k, v)


def self_body(len_ref, x_ref, o_ref, k_ref, v_ref):
    blocks, _, rows, _ = x_ref.shape
    for j in range(blocks):
        k_ref[pl.ds(j * rows, rows), :] = x_ref[j, 1]
        v_ref[pl.ds(j * rows, rows), :] = x_ref[j, 2]
    length = len_ref[0]
    for i in range(blocks):
        width = (i + 1) * rows
        scores = lax.dot_general(
            x_ref[i, 0], k_ref[:width, :], NT, preferred_element_type=F32
        ) * SCALE
        row = lax.broadcasted_iota(jnp.int32, (rows, width), 0) + i * rows
        col = lax.broadcasted_iota(jnp.int32, (rows, width), 1)
        weights = jnp.where(col <= row, jnp.exp(scores), 0.0)
        sums = jnp.dot(weights.astype(BF), v_ref[:width, :], preferred_element_type=F32)
        result = sums / jnp.sum(weights, axis=1, keepdims=True)
        place = lax.broadcasted_iota(jnp.int32, (rows, HD), 0) + i * rows
        o_ref[i] = jnp.where(place < length, result, 0.0).astype(BF)


def self_attention(lengths, x):
    blocks, _, rows, _ = x.shape
    return pl.pallas_call(
        self_body,
        out_shape=jax.ShapeDtypeStruct((blocks, rows, HD), BF),
        in_specs=[
            pl.BlockSpec(memory_space=pltpu.SMEM),
            pl.BlockSpec(memory_space=pltpu.VMEM),
        ],
        scratch_shapes=[pltpu.VMEM((blocks * rows, HD), BF)] * 2,
        name="self_attention",
    )(lengths, x)


def offer_body(ids_ref, where_ref, bank_ref, o_ref):
    peers, part = o_ref.shape[0], o_ref.shape[1]
    asks = ids_ref.shape[1] // 4
    me, piece, core = where_ref[0], where_ref[1], where_ref[2]
    for z in range(peers // 2):
        for side in range(2):
            unit = jnp.int32(0)
            for t in range(asks):
                at = side * 2 * asks + (t // NBR) * 2 * NBR + t % NBR
                unit = jnp.where(ids_ref[z, at] == me, ids_ref[z, at + NBR], unit)
            start = pl.multiple_of(unit * SPAN + piece * part, part)
            o_ref[2 * z + jnp.bitwise_xor(core, side)] = bank_ref[pl.ds(start, part), :]


def offer_rows(ids, where, bank, part):
    zs = ids.shape[0]
    return pl.pallas_call(
        offer_body,
        out_shape=jax.ShapeDtypeStruct((2 * zs, part, bank.shape[1]), bank.dtype),
        in_specs=[
            pl.BlockSpec(memory_space=pltpu.SMEM),
            pl.BlockSpec(memory_space=pltpu.SMEM),
            pl.BlockSpec(memory_space=pltpu.VMEM),
        ],
        name="offer_rows",
    )(ids, where, bank)


def choose_body(own_ref, x_ref, o_ref):
    part = x_ref.shape[1]
    for t in range(o_ref.shape[0] // part):
        o_ref[t * part : (t + 1) * part, :] = x_ref[own_ref[0, t // NBR, t % NBR]]


def choose_rows(owners, received):
    asks = owners.shape[1] * owners.shape[2]
    _, part, enc = received.shape
    return pl.pallas_call(
        choose_body,
        out_shape=jax.ShapeDtypeStruct((asks * part, enc), received.dtype),
        in_specs=[
            pl.BlockSpec(memory_space=pltpu.SMEM),
            pl.BlockSpec(memory_space=pltpu.VMEM),
        ],
        name="choose_rows",
    )(owners, received)


def stage_body(own_ref, other_ref, k_ref, v_ref, o_ref):
    copies, rows, width = o_ref.shape
    depth, half = k_ref.shape
    lane = lax.broadcasted_iota(jnp.int32, (1, HD), 1)
    spans, each = own_ref.shape[1:]
    last = jnp.zeros((1, HD), F32)
    for side, ref in enumerate((own_ref, other_ref)):
        for s in range(spans):
            for t in range(each):
                at = (side * spans + s) * each + t
                last = jnp.where(lane == at, ref[0, s, t].astype(F32), last)
    pad = jnp.zeros((rows - depth, HD), F32)
    row = lax.broadcasted_iota(jnp.int32, pad.shape, 0)
    tail = jnp.where(row == rows - depth - 1, last, pad)
    for c in range(width // HD):
        src, at = (k_ref, c * HD) if c * HD < half else (v_ref, c * HD - half)
        top = src[:, at : at + HD].astype(F32)
        end = tail if c == 0 else pad
        block = jnp.concatenate([top, end], axis=0).astype(BF)
        for n in range(copies):
            o_ref[n, :, c * HD : (c + 1) * HD] = block


def stage_weights(ids, other_ids, key_weight, value_weight, copies):
    depth, width = key_weight.shape
    rows = -(-(depth + 1) // 8) * 8
    smem, vmem = pl.BlockSpec(memory_space=pltpu.SMEM), pl.BlockSpec(memory_space=pltpu.VMEM)
    return pl.pallas_call(
        stage_body,
        out_shape=jax.ShapeDtypeStruct((copies, rows, 2 * width), BF),
        in_specs=[smem, smem, vmem, vmem],
        name="stage_weights",
    )(ids, other_ids, key_weight, value_weight)


def cross_body(pos_ref, *refs):
    piece_refs = refs[:-8]
    pick_ref, ka_ref, kb_ref, va_ref, vb_ref, q_ref, o_ref, rows_ref = refs[-8:]
    spans = q_ref.shape[1] // SPAN
    total = rows_ref.shape[0]
    each = total // spans
    half = pick_ref.shape[2]

    @pl.when(pl.program_id(0) == 0)
    def _():
        for side in range(2):
            cols = slice(side * half, (side + 1) * half)
            for p, piece in enumerate(piece_refs):
                part = jnp.dot(piece[...], pick_ref[side], preferred_element_type=F32)
                rows = part.shape[0] // spans
                for s in range(spans):
                    at = s * each + p * rows
                    rows_ref[at : at + rows, cols] = part[s * rows : (s + 1) * rows].astype(BF)

    def project(a_ref, b_ref):
        return jnp.dot(rows_ref[:, :half], a_ref[...], preferred_element_type=F32) + jnp.dot(
            rows_ref[:, half:], b_ref[...], preferred_element_type=F32
        )

    key_proj = project(ka_ref, kb_ref)
    value_proj = project(va_ref, vb_ref).astype(BF)
    start, length = pos_ref[0], pos_ref[1]
    for h in range(o_ref.shape[2] // HD):
        cols = slice(h * HD, (h + 1) * HD)
        keys = key_proj[:, cols]
        scale = lax.rsqrt(jnp.mean(keys * keys, axis=1, keepdims=True) + 1e-06)
        keys = (keys * scale).astype(BF)
        values = value_proj[:, cols]
        for s in range(spans):
            own = slice(s * each, (s + 1) * each)
            scores = lax.dot_general(
                q_ref[0, s * SPAN : (s + 1) * SPAN, cols],
                keys[own],
                NT,
                preferred_element_type=F32,
            ) * SCALE
            weights = jnp.exp(scores)
            sums = jnp.dot(weights.astype(BF), values[own], preferred_element_type=F32)
            result = sums / jnp.sum(weights, axis=1, keepdims=True)
            place = lax.broadcasted_iota(jnp.int32, (SPAN, HD), 0) + (start + s * SPAN)
            o_ref[0, s * SPAN : (s + 1) * SPAN, cols] = jnp.where(
                place < length, result, 0.0
            ).astype(BF)


def cross_attention(pos, pieces, pick, own_w, other_w, queries):
    total = sum(p.shape[0] for p in pieces)
    half, width = own_w.shape[0], own_w.shape[1] // 2
    wide = 2 * HD
    steps = width // wide
    rows = queries.shape[1]
    whole = lambda x: pl.BlockSpec(x.shape, lambda j: (0,) * x.ndim)
    key_block = pl.BlockSpec((half, wide), lambda j: (0, j))
    value_block = pl.BlockSpec((half, wide), lambda j: (0, j + steps))
    tokens = pl.BlockSpec((1, rows, wide), lambda j: (0, 0, j))
    return pl.pallas_call(
        cross_body,
        grid=(steps,),
        out_shape=jax.ShapeDtypeStruct(queries.shape, BF),
        in_specs=[
            pl.BlockSpec(memory_space=pltpu.SMEM),
            *[whole(x) for x in pieces],
            whole(pick),
            key_block,
            key_block,
            value_block,
            value_block,
            tokens,
        ],
        out_specs=tokens,
        scratch_shapes=[pltpu.VMEM((total, 2 * half), BF)],
        name="cross_attention",
    )(pos, *pieces, pick, own_w, other_w, own_w, other_w, queries)


def shift(x, axis, by):
    n = lax.axis_size(axis)
    return lax.ppermute(x, axis, [(i, (i + by) % n) for i in range(n)])


def local(
    queries,
    keys,
    values,
    cross_queries,
    encoded_bank,
    key_weight,
    value_weight,
    owner_ids,
    unit_ids,
    lengths,
):
    dp = ("z", "core")
    ctx_axes = ("x", "yl")
    core, x_at, y_at = (lax.axis_index(a) for a in ("core", "x", "yl"))
    n_z, n_x, n_y, n_mp = (lax.axis_size(a) for a in ("z", "x", "yl", "mp"))
    rows, width = queries.shape[1:]
    enc = encoded_bank.shape[3]
    asks = owner_ids.shape[1] * NBR
    part = 2 * SPAN // n_mp

    ids = jnp.concatenate([owner_ids, unit_ids], axis=2)
    staged = stage_weights(ids, shift(ids, "core", 1), key_weight, value_weight, n_z)
    depth, pad = key_weight.shape[0], staged.shape[1]
    column = lax.all_to_all(staged, "z", 0, 0, tiled=True)
    asked = column[:, pad - 1, : 4 * asks].astype(jnp.int32)

    where = jnp.stack([lax.axis_index(dp), lax.axis_index("mp"), core]).astype(jnp.int32)
    offered = offer_rows(asked, where, encoded_bank.reshape(-1, enc), part)
    received = lax.all_to_all(offered, dp, 0, 0, tiled=True)
    mine = choose_rows(owner_ids, received)
    left = shift(mine, "mp", 1)
    right = shift(mine, "mp", -1)
    far = shift(mine, "mp", 2)
    pieces = (mine, left, right, far)

    column = column.reshape(n_z * pad, 2 * width)
    beside = shift(column, "yl", 1)
    column = jnp.concatenate([column, beside], axis=0)
    w_left = shift(column, "x", 1)
    w_right = shift(column, "x", -1)
    w_far = shift(w_left, "x", 1)
    own_w = jnp.concatenate([column, w_left, w_right, w_far], axis=0)
    other_w = shift(own_w, "core", 1)

    heads = pack_heads(queries, keys, values)
    packed = lax.all_to_all(heads, ctx_axes, 0, 0, tiled=True)
    head = self_attention(lengths, packed)
    back = lax.all_to_all(head, ctx_axes, 0, 0, tiled=True)
    self_core = jnp.transpose(back, (1, 0, 2)).reshape(1, rows, width)

    half = own_w.shape[0]
    block = n_y * n_z * pad
    j = jnp.arange(half, dtype=jnp.int32)
    ring = j // block
    ahead = jnp.where(ring == 1, n_x - 1, jnp.where(ring == 2, 1, jnp.where(ring == 3, 2, 0)))
    y = jnp.bitwise_xor(y_at, (j // (n_z * pad)) & 1)
    ctx = ((x_at + ahead) & (n_x - 1)) * n_y + y
    i, z = j & (pad - 1), (j // pad) & (n_z - 1)
    dp_at = z * 2 + jnp.stack([core, 1 - core])[:, None]
    source = (dp_at * (n_x * n_y) + ctx) * depth + i
    source = jnp.where(i < depth, source, -1)
    entry = lax.broadcasted_iota(jnp.int32, (2, enc, half), 1)
    pick = (source[:, None, :] == entry).astype(BF)

    pos = jnp.stack([(x_at * n_y + y_at) * rows, lengths[0]]).astype(jnp.int32)
    cross_core = cross_attention(pos, pieces, pick, own_w, other_w, cross_queries)
    return self_core, cross_core


def solution(mesh):
    n_dp, n_ctx, n_mp = (mesh.shape[a] for a in ("dp", "ctx", "mp"))
    devices = mesh.devices.reshape(n_dp // 2, 2, n_ctx // 2, 2, n_mp)
    fine = Mesh(devices, ("z", "core", "x", "yl", "mp"))
    dp, ctx = ("z", "core"), ("x", "yl")
    tokens = P(dp, ctx, "mp")
    weight = P(dp + ctx, "mp")
    in_specs = (
        tokens,
        tokens,
        tokens,
        tokens,
        P(dp, ctx, None, None),
        weight,
        weight,
        P(dp, ctx, None),
        P(dp, ctx, None),
        P(dp),
    )
    return jax.shard_map(
        local, mesh=fine, in_specs=in_specs, out_specs=(tokens, tokens), check_vma=False
    )
```

```python
import math

import jax
import jax.numpy as jnp
from jax import lax
from jax.experimental import pallas as pl
from jax.experimental.pallas import tpu as pltpu
from jax.sharding import Mesh, PartitionSpec as P


HD = 128
SPAN = 64
NBR = 2
SCALE = 1.0 / math.sqrt(HD)
BF = jnp.bfloat16
F32 = jnp.float32
NT = (((1,), (1,)), ((), ()))


def pack_body(q_ref, k_ref, v_ref, o_ref):
    for h in range(o_ref.shape[0]):
        cols = slice(h * HD, (h + 1) * HD)
        o_ref[h, 0] = q_ref[0, :, cols]
        o_ref[h, 1] = k_ref[0, :, cols]
        o_ref[h, 2] = v_ref[0, :, cols]


def pack_heads(q, k, v):
    rows, width = q.shape[1:]
    return pl.pallas_call(
        pack_body,
        out_shape=jax.ShapeDtypeStruct((width // HD, 3, rows, HD), q.dtype),
        name="pack_heads",
    )(q, k, v)


def self_body(len_ref, x_ref, o_ref, k_ref, v_ref):
    blocks, _, rows, _ = x_ref.shape
    for j in range(blocks):
        k_ref[pl.ds(j * rows, rows), :] = x_ref[j, 1]
        v_ref[pl.ds(j * rows, rows), :] = x_ref[j, 2]
    length = len_ref[0]
    for i in range(blocks):
        width = (i + 1) * rows
        scores = lax.dot_general(
            x_ref[i, 0], k_ref[:width, :], NT, preferred_element_type=F32
        ) * SCALE
        row = lax.broadcasted_iota(jnp.int32, (rows, width), 0) + i * rows
        col = lax.broadcasted_iota(jnp.int32, (rows, width), 1)
        weights = jnp.where(col <= row, jnp.exp(scores), 0.0)
        sums = jnp.dot(weights.astype(BF), v_ref[:width, :], preferred_element_type=F32)
        result = sums / jnp.sum(weights, axis=1, keepdims=True)
        place = lax.broadcasted_iota(jnp.int32, (rows, HD), 0) + i * rows
        o_ref[i] = jnp.where(place < length, result, 0.0).astype(BF)


def self_attention(lengths, x):
    blocks, _, rows, _ = x.shape
    return pl.pallas_call(
        self_body,
        out_shape=jax.ShapeDtypeStruct((blocks, rows, HD), BF),
        in_specs=[
            pl.BlockSpec(memory_space=pltpu.SMEM),
            pl.BlockSpec(memory_space=pltpu.VMEM),
        ],
        scratch_shapes=[pltpu.VMEM((blocks * rows, HD), BF)] * 2,
        name="self_attention",
    )(lengths, x)


def offer_body(ids_ref, where_ref, bank_ref, o_ref):
    peers, part = o_ref.shape[0], o_ref.shape[1]
    asks = ids_ref.shape[1] // 4
    me, piece, core = where_ref[0], where_ref[1], where_ref[2]
    for z in range(peers // 2):
        for side in range(2):
            unit = jnp.int32(0)
            for t in range(asks):
                at = side * 2 * asks + (t // NBR) * 2 * NBR + t % NBR
                unit = jnp.where(ids_ref[z, at] == me, ids_ref[z, at + NBR], unit)
            start = pl.multiple_of(unit * SPAN + piece * part, part)
            o_ref[2 * z + jnp.bitwise_xor(core, side)] = bank_ref[pl.ds(start, part), :]


def offer_rows(ids, where, bank, part):
    zs = ids.shape[0]
    return pl.pallas_call(
        offer_body,
        out_shape=jax.ShapeDtypeStruct((2 * zs, part, bank.shape[1]), bank.dtype),
        in_specs=[
            pl.BlockSpec(memory_space=pltpu.SMEM),
            pl.BlockSpec(memory_space=pltpu.SMEM),
            pl.BlockSpec(memory_space=pltpu.VMEM),
        ],
        name="offer_rows",
    )(ids, where, bank)


def choose_body(own_ref, x_ref, o_ref):
    part = x_ref.shape[1]
    for t in range(o_ref.shape[0] // part):
        o_ref[t * part : (t + 1) * part, :] = x_ref[own_ref[0, t // NBR, t % NBR]]


def choose_rows(owners, received):
    asks = owners.shape[1] * owners.shape[2]
    _, part, enc = received.shape
    return pl.pallas_call(
        choose_body,
        out_shape=jax.ShapeDtypeStruct((asks * part, enc), received.dtype),
        in_specs=[
            pl.BlockSpec(memory_space=pltpu.SMEM),
            pl.BlockSpec(memory_space=pltpu.VMEM),
        ],
        name="choose_rows",
    )(owners, received)


def stage_body(own_ref, other_ref, k_ref, v_ref, o_ref):
    copies, rows, width = o_ref.shape
    depth, half = k_ref.shape
    lane = lax.broadcasted_iota(jnp.int32, (1, HD), 1)
    spans, each = own_ref.shape[1:]
    last = jnp.zeros((1, HD), F32)
    for side, ref in enumerate((own_ref, other_ref)):
        for s in range(spans):
            for t in range(each):
                at = (side * spans + s) * each + t
                last = jnp.where(lane == at, ref[0, s, t].astype(F32), last)
    pad = jnp.zeros((rows - depth, HD), F32)
    row = lax.broadcasted_iota(jnp.int32, pad.shape, 0)
    tail = jnp.where(row == rows - depth - 1, last, pad)
    for c in range(width // HD):
        src, at = (k_ref, c * HD) if c * HD < half else (v_ref, c * HD - half)
        top = src[:, at : at + HD].astype(F32)
        end = tail if c == 0 else pad
        block = jnp.concatenate([top, end], axis=0).astype(BF)
        for n in range(copies):
            o_ref[n, :, c * HD : (c + 1) * HD] = block


def stage_weights(ids, other_ids, key_weight, value_weight, copies):
    depth, width = key_weight.shape
    rows = -(-(depth + 1) // 8) * 8
    smem, vmem = pl.BlockSpec(memory_space=pltpu.SMEM), pl.BlockSpec(memory_space=pltpu.VMEM)
    return pl.pallas_call(
        stage_body,
        out_shape=jax.ShapeDtypeStruct((copies, rows, 2 * width), BF),
        in_specs=[smem, smem, vmem, vmem],
        name="stage_weights",
    )(ids, other_ids, key_weight, value_weight)


def cross_body(pos_ref, *refs):
    piece_refs = refs[:-8]
    pick_ref, ka_ref, kb_ref, va_ref, vb_ref, q_ref, o_ref, rows_ref = refs[-8:]
    spans = q_ref.shape[1] // SPAN
    total = rows_ref.shape[0]
    each = total // spans
    half = pick_ref.shape[2]

    @pl.when(pl.program_id(0) == 0)
    def _():
        for side in range(2):
            cols = slice(side * half, (side + 1) * half)
            for p, piece in enumerate(piece_refs):
                part = jnp.dot(piece[...], pick_ref[side], preferred_element_type=F32)
                rows = part.shape[0] // spans
                for s in range(spans):
                    at = s * each + p * rows
                    rows_ref[at : at + rows, cols] = part[s * rows : (s + 1) * rows].astype(BF)

    def project(a_ref, b_ref):
        return jnp.dot(rows_ref[:, :half], a_ref[...], preferred_element_type=F32) + jnp.dot(
            rows_ref[:, half:], b_ref[...], preferred_element_type=F32
        )

    key_proj = project(ka_ref, kb_ref)
    heads = [slice(h * HD, (h + 1) * HD) for h in range(o_ref.shape[2] // HD)]
    keys = []
    for cols in heads:
        head = key_proj[:, cols]
        scale = lax.rsqrt(jnp.mean(head * head, axis=1, keepdims=True) + 1e-06)
        keys.append((head * scale).astype(BF))
    values = project(va_ref, vb_ref).astype(BF)
    start, length = pos_ref[0], pos_ref[1]
    places = [(h, s) for h in range(len(heads)) for s in range(spans)]
    token = lambda s: slice(s * SPAN, (s + 1) * SPAN)
    own = lambda s: slice(s * each, (s + 1) * each)
    weights = [
        jnp.exp(
            lax.dot_general(
                q_ref[0, token(s), heads[h]], keys[h][own(s)], NT, preferred_element_type=F32
            )
            * SCALE
        )
        for h, s in places
    ]
    sums = [
        jnp.dot(w.astype(BF), values[own(s), heads[h]], preferred_element_type=F32)
        for w, (h, s) in zip(weights, places)
    ]
    totals = [jnp.sum(w, axis=1, keepdims=True) for w in weights]
    for top, total_weight, (h, s) in zip(sums, totals, places):
        place = lax.broadcasted_iota(jnp.int32, (SPAN, HD), 0) + (start + s * SPAN)
        o_ref[0, token(s), heads[h]] = jnp.where(
            place < length, top / total_weight, 0.0
        ).astype(BF)


def cross_attention(pos, pieces, pick, own_w, other_w, queries):
    total = sum(p.shape[0] for p in pieces)
    half, width = own_w.shape[0], own_w.shape[1] // 2
    wide = 2 * HD
    steps = width // wide
    rows = queries.shape[1]
    whole = lambda x: pl.BlockSpec(x.shape, lambda j: (0,) * x.ndim)
    key_block = pl.BlockSpec((half, wide), lambda j: (0, j))
    value_block = pl.BlockSpec((half, wide), lambda j: (0, j + steps))
    tokens = pl.BlockSpec((1, rows, wide), lambda j: (0, 0, j))
    return pl.pallas_call(
        cross_body,
        grid=(steps,),
        out_shape=jax.ShapeDtypeStruct(queries.shape, BF),
        in_specs=[
            pl.BlockSpec(memory_space=pltpu.SMEM),
            *[whole(x) for x in pieces],
            whole(pick),
            key_block,
            key_block,
            value_block,
            value_block,
            tokens,
        ],
        out_specs=tokens,
        scratch_shapes=[pltpu.VMEM((total, 2 * half), BF)],
        name="cross_attention",
    )(pos, *pieces, pick, own_w, other_w, own_w, other_w, queries)


def shift(x, axis, by):
    n = lax.axis_size(axis)
    return lax.ppermute(x, axis, [(i, (i + by) % n) for i in range(n)])


def local(
    queries,
    keys,
    values,
    cross_queries,
    encoded_bank,
    key_weight,
    value_weight,
    owner_ids,
    unit_ids,
    lengths,
):
    dp = ("z", "core")
    ctx_axes = ("x", "yl")
    core, x_at, y_at = (lax.axis_index(a) for a in ("core", "x", "yl"))
    n_z, n_x, n_y, n_mp = (lax.axis_size(a) for a in ("z", "x", "yl", "mp"))
    rows, width = queries.shape[1:]
    enc = encoded_bank.shape[3]
    asks = owner_ids.shape[1] * NBR
    part = 2 * SPAN // n_mp

    ids = jnp.concatenate([owner_ids, unit_ids], axis=2)
    staged = stage_weights(ids, shift(ids, "core", 1), key_weight, value_weight, n_z)
    depth, pad = key_weight.shape[0], staged.shape[1]
    column = lax.all_to_all(staged, "z", 0, 0, tiled=True)
    asked = column[:, pad - 1, : 4 * asks].astype(jnp.int32)

    where = jnp.stack([lax.axis_index(dp), lax.axis_index("mp"), core]).astype(jnp.int32)
    offered = offer_rows(asked, where, encoded_bank.reshape(-1, enc), part)
    received = lax.all_to_all(offered, dp, 0, 0, tiled=True)
    mine = choose_rows(owner_ids, received)
    left = shift(mine, "mp", 1)
    right = shift(mine, "mp", -1)
    far = shift(mine, "mp", 2)
    pieces = (mine, left, right, far)

    column = column.reshape(n_z * pad, 2 * width)
    beside = shift(column, "yl", 1)
    column = jnp.concatenate([column, beside], axis=0)
    w_left = shift(column, "x", 1)
    w_right = shift(column, "x", -1)
    w_far = shift(w_left, "x", 1)
    heads = pack_heads(queries, keys, values)
    packed = lax.all_to_all(heads, ctx_axes, 0, 0, tiled=True)
    head = self_attention(lengths, packed)
    column, w_left, w_right, head = lax.optimization_barrier((column, w_left, w_right, head))
    own_w = jnp.concatenate([column, w_left, w_right, w_far], axis=0)
    other_w = shift(own_w, "core", 1)
    back = lax.all_to_all(head, ctx_axes, 0, 0, tiled=True)
    self_core = jnp.transpose(back, (1, 0, 2)).reshape(1, rows, width)

    half = own_w.shape[0]
    block = n_y * n_z * pad
    j = jnp.arange(half, dtype=jnp.int32)
    ring = j // block
    ahead = jnp.where(ring == 1, n_x - 1, jnp.where(ring == 2, 1, jnp.where(ring == 3, 2, 0)))
    y = jnp.bitwise_xor(y_at, (j // (n_z * pad)) & 1)
    ctx = ((x_at + ahead) & (n_x - 1)) * n_y + y
    i, z = j & (pad - 1), (j // pad) & (n_z - 1)
    dp_at = z * 2 + jnp.stack([core, 1 - core])[:, None]
    source = (dp_at * (n_x * n_y) + ctx) * depth + i
    source = jnp.where(i < depth, source, -1)
    entry = lax.broadcasted_iota(jnp.int32, (2, enc, half), 1)
    pick = (source[:, None, :] == entry).astype(BF)

    pos = jnp.stack([(x_at * n_y + y_at) * rows, lengths[0]]).astype(jnp.int32)
    cross_core = cross_attention(pos, pieces, pick, own_w, other_w, cross_queries)
    return self_core, cross_core


def solution(mesh):
    n_dp, n_ctx, n_mp = (mesh.shape[a] for a in ("dp", "ctx", "mp"))
    devices = mesh.devices.reshape(n_dp // 2, 2, n_ctx // 2, 2, n_mp)
    fine = Mesh(devices, ("z", "core", "x", "yl", "mp"))
    dp, ctx = ("z", "core"), ("x", "yl")
    tokens = P(dp, ctx, "mp")
    weight = P(dp + ctx, "mp")
    in_specs = (
        tokens,
        tokens,
        tokens,
        tokens,
        P(dp, ctx, None, None),
        weight,
        weight,
        P(dp, ctx, None),
        P(dp, ctx, None),
        P(dp),
    )
    return jax.shard_map(
        local, mesh=fine, in_specs=in_specs, out_specs=(tokens, tokens), check_vma=False
    )
```
